256 devices in a mesh: expert: 16 (over y, x), tensor: 16 (over z, core).
Axes of the slice: x: 4, y: 4, z: 8, core: 2. Of those that a mesh axis runs over, the one named last changes fastest.
Arguments:
- queries: bfloat16 [4096, 8192], P('expert', 'tensor'), may hold values from -8 to 8
- keys_values: bfloat16 [16, 4, 1280, 256], P('expert'), may hold values from -6 to 6
- prefix_len: int32 [16], P('expert'), may hold values from 128 to 1024, as said below
- out_proj: bfloat16 [8192, 4096], P('tensor', 'expert'), may hold values from -0.0625 to 0.0625
- residual: bfloat16 [4096, 4096], P(('expert', 'tensor')), may hold values from -1.796875 to 1.796875
- norm_gain: float32 [4096], replicated, may hold values from 0.1 to 1.9
- expert_ids: int32 [4096, 8], P('expert'), may hold values from 0 to 63, all different within a row; in each aligned block of 16 rows (0 to 15, 16 to 31, ...) at most 3 rows name the same one
- route_weights: bfloat16 [4096, 8], P('expert'), may hold values from 0.19921875 to 1
- w_gate: bfloat16 [256, 4096, 384], P(('expert', 'tensor')), may hold values from -0.09375 to 0.09375
- w_up: bfloat16 [256, 4096, 384], P(('expert', 'tensor')), may hold values from -0.09375 to 0.09375
- w_down: bfloat16 [256, 384, 4096], P(('expert', 'tensor')), may hold values from -0.15625 to 0.15625
Outputs:
- layer_out: bfloat16 [4096, 4096], P(('expert', 'tensor'))
The draws below stay inside these ranges and needn't reach their ends.
Inputs may be any that keep to these rules, and one draw needn't show every extreme that they name: `expert_ids`: in the rows of one device (aligned blocks of 16 rows) no expert is named by more than 3 rows, a bound that some block reaches; a row names 8 different experts. `prefix_len`: some sequence has all 1024 slots live.
All inputs are finite; a program needn't handle non-finite values.
Results may differ from the reference program's by a relative error of at most 0.035.
Values may be sent and summed in bfloat16 or wider, within the bound.
No kernel may reach another device: no remote copies, remote signals or barrier semaphores. Data moves between devices by JAX's collectives and lax.ppermute only.
A program may use at most 128 MiB of HBM per device.

```python
import math
import jax
import jax.numpy as jnp
import numpy as np
from jax import lax

D = 4096
HEADS = 64
KVH = 4
HD = 128
FFE = 1536
TOPK = 8
HSPLIT = 4
TOK_DEV = 16
PREFIX = 1024
EXPERTS = 64
QH = 384
STEP_TOKENS = 256
CTX = 1280
TOKENS = 4096
MOST = 3
CAP = 48
N_EXPERT = 16
N_TENSOR = 16


def attention_pair(key):
    joint = jax.random.fold_in(key, 11)
    first_key, second_key = jax.random.split(joint, 2)
    query_all = jnp.clip(2.0 * jax.random.normal(first_key, (N_EXPERT * STEP_TOKENS, HEADS * HD), jnp.float32), -8.0, 8.0)
    cached = jnp.clip(jax.random.normal(second_key, (N_EXPERT, KVH, CTX, 2 * HD), jnp.float32), -6.0, 6.0)
    return (query_all, cached)


def draw_queries(key, part):
    return attention_pair(key)[0].astype(jnp.bfloat16)


def draw_keys_values(key, part):
    return attention_pair(key)[1].astype(jnp.bfloat16)


def draw_prefix_len(key, part):
    length_key, pick_key = jax.random.split(jax.random.fold_in(key, 23))
    lengths = jax.random.randint(length_key, (N_EXPERT,), PREFIX // 8, PREFIX + 1)
    longest = jax.random.randint(pick_key, (), 0, N_EXPERT)
    return jnp.where(jnp.arange(N_EXPERT) == longest, PREFIX, lengths).astype(jnp.int32)


def block_levels(own_key, dims, pieces, smallest, top_value):
    factor_of, own = 1.0, jax.random.fold_in(own_key, 6)
    for position, parts in pieces:
        heights = jnp.exp(jax.random.uniform(jax.random.fold_in(own, position), (parts,), jnp.float32, smallest / len(pieces), top_value / len(pieces)))
        factor_of = factor_of * jnp.repeat(heights, dims[position] // parts).reshape([-1 if axis == position else 1 for axis in range(len(dims))])
    return factor_of


def assign_block(own_key, own, number, rows, amount, top, reach, lean):
    ranking = jax.random.permutation(own_key, amount)
    crowded, ordinary = portions_of(amount, rows * top, reach, lean, True), portions_of(amount, rows * top, reach, lean, False)
    places = jnp.arange(amount)

    def named(sizes, offset_by):
        used = int((sizes > 0).sum())
        fixed = max(1, used // 4)
        shifted = fixed + (places - fixed + offset_by * (used - fixed)) % max(1, amount - fixed)
        return jnp.zeros((amount,), jnp.int32).at[ranking[jnp.where(places < fixed, places, shifted)]].set(jnp.asarray(sizes, jnp.int32))

    sizes = jnp.where(number % 4 == 0, named(crowded, number // 4), named(ordinary, number - number // 4 - 1))
    mixed = jax.random.permutation(jax.random.fold_in(own, 3), amount)
    giver, sink = mixed[0:amount // 2 * 2:2], mixed[1:amount // 2 * 2:2]
    room = jnp.minimum(sizes[giver] - 1, reach - sizes[sink]) // 2
    room = jnp.where((giver == ranking[0]) | (sink == ranking[0]) | (sizes[sink] == 0), 0, jnp.maximum(room, 0))
    shifted = jax.random.randint(jax.random.fold_in(own, 4), (amount // 2,), 0, 1 << 20) % (room + 1)
    sizes = sizes.at[giver].add(-shifted).at[sink].add(shifted)
    members = jnp.searchsorted(jnp.cumsum(sizes), jnp.arange(rows * top), side="right").astype(jnp.int32)
    listing = members.reshape(top, rows).T
    listing = listing[jax.random.permutation(jax.random.fold_in(own, 1), rows)]
    offset_by = jax.random.randint(jax.random.fold_in(own, 2), (rows, 1), 0, top)
    return jnp.take_along_axis(listing, (jnp.arange(top)[None, :] + offset_by) % top, axis=1)


def portions_of(count, total, reach, lean, full):
    loads = [(1 << 20) // math.isqrt(standing ** lean) + 1 for standing in range(1, count + 1)]
    largest = reach if full else min(reach, max(-(-total // count), total * loads[0] // sum(loads)))
    least = 1 if total - largest >= count - 1 else 0
    counts, spare = [largest] + [least] * (count - 1), total - largest - least * (count - 1)
    while spare > 0:
        movable = [i for i in range(1, count) if counts[i] < largest] or [i for i in range(1, count) if counts[i] < reach]
        whole, remaining = sum([loads[i] for i in movable]), spare
        for i in movable:
            more = min(reach - counts[i], max(1, remaining * loads[i] // whole), spare)
            counts[i] = counts[i] + more
            spare = spare - more
    return np.array(counts)


def scatter_about(stream_key, shape, spread, reach, shards=(), kind=jnp.bfloat16):
    factor_of = block_levels(stream_key, shape, shards, -0.22, 0.18) if shards else 1.0
    values = jax.random.normal(stream_key, shape, jnp.float32) * spread * factor_of
    return jnp.minimum(jnp.maximum(values, -reach), reach).astype(kind)


def setup_inputs(seed: int = 0) -> dict:
    key_list = jax.random.split(jax.random.key(seed), 12)
    queries = draw_queries(jax.random.fold_in(key_list[11], 71), 0)
    keys_values = draw_keys_values(jax.random.fold_in(key_list[11], 71), 0)
    prefix_len = draw_prefix_len(jax.random.fold_in(key_list[11], 71), 0)
    out_proj = scatter_about(key_list[3], (HEADS * HD, D), (HEADS * HD) ** -0.5, 0.0625, ((0, 16), (1, 16)))
    residual = scatter_about(key_list[4], (TOKENS, D), 0.3, 1.796875, ((0, 256),))
    norm_gain = jnp.clip(1.0 + 0.18 * jax.random.normal(key_list[5], (D,), jnp.float32), 0.1, 1.9)
    expert_ids_keys = jax.random.split(jax.random.fold_in(key_list[6], 1), TOKENS // TOK_DEV)
    expert_ids_turns = jax.random.permutation(jax.random.fold_in(key_list[6], 3), TOKENS // TOK_DEV)
    expert_ids = jax.vmap(lambda own, number: assign_block(jax.random.fold_in(key_list[6], 2), own, number, TOK_DEV, EXPERTS, TOPK, MOST, 2))(expert_ids_keys, expert_ids_turns).reshape((TOKENS, TOPK))
    route_weights = jnp.clip(0.19921875 + 0.80078125 * jax.random.uniform(key_list[7], (TOKENS, TOPK), jnp.float32) ** block_levels(key_list[7], (TOKENS, TOPK), ((0, 16),), -0.2, 0.2), 0.19921875, 1.0).astype(jnp.bfloat16)
    w_gate = scatter_about(key_list[8], (EXPERTS * HSPLIT, D, QH), D ** -0.5, 0.09375, ((0, 256),))
    w_up = scatter_about(key_list[9], (EXPERTS * HSPLIT, D, QH), D ** -0.5, 0.09375, ((0, 256),))
    w_down = scatter_about(key_list[10], (EXPERTS * HSPLIT, QH, D), FFE ** -0.5, 0.15625, ((0, 256),))
    return {"queries": queries, "keys_values": keys_values, "prefix_len": prefix_len, "out_proj": out_proj, "residual": residual, "norm_gain": norm_gain, "expert_ids": expert_ids, "route_weights": route_weights, "w_gate": w_gate, "w_up": w_up, "w_down": w_down}


def reference(queries, keys_values, prefix_len, out_proj, residual, norm_gain, expert_ids, route_weights, w_gate, w_up, w_down):
    group_size = HEADS // KVH
    per_device = HEADS // N_TENSOR
    projection = out_proj.astype(jnp.float32).reshape(N_TENSOR, per_device * HD, D)

    def one_sequence(sequence):
        query_rows = lax.dynamic_slice_in_dim(queries, sequence * STEP_TOKENS, STEP_TOKENS, 0).astype(jnp.float32)
        query_rows = query_rows.reshape(STEP_TOKENS, KVH, group_size, HD)
        cached = lax.dynamic_index_in_dim(keys_values, sequence, 0, keepdims=False).astype(jnp.float32)
        key_rows = cached[:, :, :HD]
        value_rows = cached[:, :, HD:]
        scores = jnp.einsum('ngqd,gcd->gqnc', query_rows, key_rows) / math.sqrt(HD)
        length = lax.dynamic_index_in_dim(prefix_len, sequence, 0, keepdims=False)
        columns = jnp.arange(CTX, dtype=jnp.int32)[None, :]
        positions = jnp.arange(STEP_TOKENS, dtype=jnp.int32)[:, None]
        visible = ((columns < length) | (columns >= PREFIX) & (columns - PREFIX <= positions))[None, None]
        highest = lax.optimization_barrier(jnp.max(jnp.where(visible, scores, -1e+30), axis=-1, keepdims=True))
        weights = jnp.exp(jnp.where(visible, scores - highest, -1e+30))
        summed = lax.optimization_barrier(jnp.sum(weights, axis=-1))
        rounded = lax.optimization_barrier(weights.astype(jnp.bfloat16)).astype(jnp.float32)
        blended = jnp.einsum('gqnc,gcd->ngqd', rounded, value_rows)
        blended = blended / jnp.transpose(summed, (2, 0, 1))[:, :, :, None]
        attended = blended.reshape(STEP_TOKENS, HEADS * HD).astype(jnp.bfloat16)
        head_parts = jnp.einsum('ntk,tkd->tnd', attended.astype(jnp.float32).reshape(STEP_TOKENS, N_TENSOR, per_device * HD), projection)
        head_parts = lax.optimization_barrier(head_parts.astype(jnp.bfloat16)).astype(jnp.float32)
        rows_in = lax.dynamic_slice_in_dim(residual, sequence * STEP_TOKENS, STEP_TOKENS, 0).astype(jnp.float32)
        return (rows_in + lax.optimization_barrier(jnp.sum(head_parts, axis=0))).astype(jnp.bfloat16)
    hidden_state = lax.map(one_sequence, jnp.arange(N_EXPERT, dtype=jnp.int32)).reshape(TOKENS, D)
    values = hidden_state.astype(jnp.float32)
    normed = values * lax.rsqrt(lax.optimization_barrier(jnp.mean(values * values, axis=-1, keepdims=True)) + 1e-06) * norm_gain[None, :]
    normed = normed.astype(jnp.bfloat16)
    row_ids = jnp.arange(TOKENS, dtype=jnp.int32)
    named_mask = expert_ids[:, :, None] == jnp.arange(EXPERTS, dtype=jnp.int32)[None, None, :]
    hit_table = lax.optimization_barrier(jnp.sum(named_mask.astype(jnp.int32), axis=1)).astype(jnp.int32)
    weight_table = lax.optimization_barrier(jnp.sum(jnp.where(named_mask, route_weights[:, :, None].astype(jnp.float32), 0.0), axis=1))
    grouped = hit_table.reshape(TOKENS // TOK_DEV, TOK_DEV, EXPERTS)
    rank_table = (jnp.cumsum(grouped, axis=1) - grouped).reshape(TOKENS, EXPERTS).astype(jnp.int32)
    slot_column = ((row_ids // STEP_TOKENS)[:, None] * CAP + (row_ids // TOK_DEV % N_TENSOR)[:, None] * MOST + rank_table).astype(jnp.int32)
    expert_column = jnp.where(hit_table == 1, jnp.arange(EXPERTS, dtype=jnp.int32)[None, :], EXPERTS).astype(jnp.int32)
    source_table = jnp.full((EXPERTS, N_EXPERT * CAP), TOKENS, jnp.int32)
    source_table = source_table.at[expert_column.reshape(-1), slot_column.reshape(-1)].set(jnp.broadcast_to(row_ids[:, None], (TOKENS, EXPERTS)).reshape(-1), mode='drop')
    gain_table = jnp.zeros((EXPERTS, N_EXPERT * CAP), jnp.float32)
    gain_table = gain_table.at[expert_column.reshape(-1), slot_column.reshape(-1)].set(weight_table.reshape(-1), mode='drop')

    def one_expert(accumulated, expert):
        expert = expert.astype(jnp.int32)
        sources = lax.dynamic_index_in_dim(source_table, expert, 0, keepdims=False)
        gain_row = lax.dynamic_index_in_dim(gain_table, expert, 0, keepdims=False)
        inputs = jnp.take(normed, jnp.minimum(sources, TOKENS - 1), axis=0)
        total = jnp.zeros((N_EXPERT * CAP, D), jnp.float32)
        for quarter in range(HSPLIT):
            weight_row = (expert * HSPLIT + quarter).astype(jnp.int32)
            gate_w = lax.dynamic_index_in_dim(w_gate, weight_row, 0, keepdims=False)
            up_w = lax.dynamic_index_in_dim(w_up, weight_row, 0, keepdims=False)
            down_w = lax.dynamic_index_in_dim(w_down, weight_row, 0, keepdims=False)
            gate_val = jnp.dot(inputs, gate_w, preferred_element_type=jnp.float32)
            up_val = jnp.dot(inputs, up_w, preferred_element_type=jnp.float32)
            inner = (jax.nn.silu(gate_val) * up_val).astype(jnp.bfloat16)
            result = jnp.dot(inner, down_w, preferred_element_type=jnp.float32).astype(jnp.bfloat16)
            result = lax.optimization_barrier(result).astype(jnp.float32)
            total = total + gain_row[:, None] * result
        accumulated = accumulated.at[sources].add(total, mode='drop')
        return (accumulated, None)
    expert_sum, _ = lax.scan(one_expert, jnp.zeros((TOKENS, D), jnp.float32), jnp.arange(EXPERTS, dtype=jnp.int32))
    return (hidden_state.astype(jnp.float32) + expert_sum).astype(jnp.bfloat16)
```

```python
import math

import jax
import jax.numpy as jnp
from jax import lax
from jax.sharding import PartitionSpec as P

HEADS = 64
KVH = 4
HD = 128
TOPK = 8
HSPLIT = 4
TOK_DEV = 16
PREFIX = 1024
MOST = 3

F32 = jnp.float32
BF16 = jnp.bfloat16


def chip_swap(array, tensor_count):
    return lax.ppermute(array, "tensor", [(t, t ^ 1) for t in range(tensor_count)])


def along_z(array, groups):
    return lax.all_to_all(
        array, "tensor", split_axis=0, concat_axis=0, tiled=True, axis_index_groups=groups
    )


def attend(queries, keys_values, prefix_len, kv_index):
    step_rows = queries.shape[0]
    per_device = queries.shape[1] // HD
    cached = lax.dynamic_index_in_dim(keys_values[0], kv_index, 0, keepdims=False)
    key_rows = cached[:, :HD]
    value_rows = cached[:, HD:]
    context = cached.shape[0]
    query_rows = queries.reshape(step_rows, per_device, HD)
    scores = jnp.einsum("nhd,cd->hnc", query_rows, key_rows, preferred_element_type=F32) / math.sqrt(HD)
    columns = jnp.arange(context, dtype=jnp.int32)[None, :]
    positions = jnp.arange(step_rows, dtype=jnp.int32)[:, None]
    visible = ((columns < prefix_len[0]) | (columns >= PREFIX) & (columns - PREFIX <= positions))[None]
    highest = jnp.max(jnp.where(visible, scores, -1e30), axis=-1, keepdims=True)
    weights = jnp.exp(jnp.where(visible, scores - highest, -1e30))
    summed = jnp.sum(weights, axis=-1)
    blended = jnp.einsum("hnc,cd->nhd", weights.astype(BF16), value_rows, preferred_element_type=F32)
    attended = (blended / jnp.transpose(summed)[:, :, None]).astype(BF16)
    return attended.reshape(step_rows, per_device * HD)


def shards(
    queries,
    keys_values,
    prefix_len,
    out_proj,
    residual,
    norm_gain,
    expert_ids,
    route_weights,
    w_gate,
    w_up,
    w_down,
):
    tensor_count = lax.axis_size("tensor")
    expert_count = lax.axis_size("expert")
    tensor_index = lax.axis_index("tensor")
    chips = tensor_count // 2
    core = tensor_index % 2
    same_core = [[2 * z + c for z in range(chips)] for c in range(2)]
    per_device = queries.shape[1] // HD
    width = residual.shape[1]
    half_rows = chips * TOK_DEV

    gate_other = chip_swap(w_gate[0], tensor_count)
    up_other = chip_swap(w_up[0], tensor_count)
    down_other = chip_swap(w_down[0], tensor_count)

    slot_index = tensor_index // HSPLIT
    slot_count = tensor_count // HSPLIT
    capacity = chips * MOST
    ids = expert_ids.reshape(chips, 2, TOK_DEV, TOPK)
    ids = lax.dynamic_index_in_dim(ids, core, 1, keepdims=False)
    gains = route_weights.reshape(chips, 2, TOK_DEV, TOPK)
    gains = lax.dynamic_index_in_dim(gains, core, 1, keepdims=False)
    wanted = jnp.arange(expert_count, dtype=jnp.int32) * slot_count + slot_index
    named = ids[:, :, :, None] == wanted
    hits = jnp.sum(named.astype(jnp.int32), axis=2)
    weight = jnp.sum(jnp.where(named, gains[:, :, :, None].astype(F32), 0.0), axis=2)
    earlier = (jnp.arange(TOK_DEV)[:, None] > jnp.arange(TOK_DEV)[None, :]).astype(BF16)
    rank = jnp.einsum("nm,zmj->znj", earlier, hits.astype(BF16), preferred_element_type=F32)
    position = jnp.arange(chips, dtype=jnp.int32)[:, None, None] * MOST + rank.astype(jnp.int32)
    position = jnp.where(hits > 0, position, -1).reshape(half_rows, expert_count)
    weight = weight.reshape(half_rows, expert_count)
    slots = jnp.arange(capacity, dtype=jnp.int32)
    pick = (position.T[:, None, :] == slots[None, :, None]).astype(BF16)
    pick = pick.reshape(expert_count * capacity, half_rows)
    combine = jnp.where(position[:, :, None] == slots[None, None, :], weight[:, :, None], 0.0)
    combine = combine.astype(BF16).reshape(half_rows, expert_count * capacity)

    attended = attend(queries, keys_values, prefix_len, tensor_index * per_device // (HEADS // KVH))
    projection = lax.all_gather(out_proj, "expert", axis=1, tiled=True)
    attended = attended.reshape(chips, 2, TOK_DEV, per_device * HD)
    attended_away = lax.dynamic_index_in_dim(attended, 1 - core, 1, keepdims=False)
    attended_here = lax.dynamic_index_in_dim(attended, core, 1, keepdims=False)
    part_away = jnp.dot(attended_away.reshape(half_rows, -1), projection, preferred_element_type=F32).astype(BF16)
    part_away = chip_swap(part_away, tensor_count)
    part_here = jnp.dot(attended_here.reshape(half_rows, -1), projection, preferred_element_type=F32).astype(BF16)
    chip_part = (part_here.astype(F32) + part_away.astype(F32)).astype(BF16)
    head_parts = along_z(chip_part.reshape(chips, TOK_DEV, width), same_core)
    head_sum = jnp.sum(head_parts.astype(F32), axis=0)
    hidden_state = (residual.astype(F32) + head_sum).astype(BF16)

    values = hidden_state.astype(F32)
    factor = lax.rsqrt(jnp.mean(values * values, axis=-1, keepdims=True) + 1e-06)
    normed = (values * factor * norm_gain[None, :]).astype(BF16)
    normed_half = along_z(jnp.broadcast_to(normed[None], (chips,) + normed.shape), same_core)

    outgoing = jnp.dot(pick, normed_half.reshape(half_rows, width), preferred_element_type=F32).astype(BF16)
    arrived = lax.all_to_all(
        outgoing.reshape(expert_count, capacity, width), "expert", split_axis=0, concat_axis=0, tiled=True
    )
    rows = arrived.reshape(expert_count * capacity, width)

    def inner_of(gate, up):
        gate_val = jnp.dot(rows, gate, preferred_element_type=F32)
        up_val = jnp.dot(rows, up, preferred_element_type=F32)
        return (jax.nn.silu(gate_val) * up_val).astype(BF16)

    result = jnp.dot(inner_of(w_gate[0], w_up[0]), w_down[0], preferred_element_type=F32)
    result = result + jnp.dot(inner_of(gate_other, up_other), down_other, preferred_element_type=F32)
    result = result.astype(BF16).reshape(expert_count, capacity, width)
    returned = lax.all_to_all(result, "expert", split_axis=0, concat_axis=0, tiled=True)
    expert_part = jnp.dot(combine, returned.reshape(expert_count * capacity, width), preferred_element_type=F32)
    expert_parts = along_z(expert_part.astype(BF16).reshape(chips, TOK_DEV, width), same_core)
    expert_sum = jnp.sum(expert_parts.astype(F32), axis=0)
    return (hidden_state.astype(F32) + expert_sum).astype(BF16)


def solution(mesh):
    return jax.shard_map(
        shards,
        mesh=mesh,
        in_specs=(
            P("expert", "tensor"),
            P("expert", None, None, None),
            P("expert"),
            P("tensor", "expert"),
            P(("expert", "tensor"), None),
            P(),
            P("expert", None),
            P("expert", None),
            P(("expert", "tensor"), None, None),
            P(("expert", "tensor"), None, None),
            P(("expert", "tensor"), None, None),
        ),
        out_specs=P(("expert", "tensor"), None),
        check_vma=False,
    )
```

```python
import math

import jax
import jax.numpy as jnp
from jax import lax
from jax.sharding import PartitionSpec as P

HEADS = 64
KVH = 4
HD = 128
TOPK = 8
HSPLIT = 4
TOK_DEV = 16
PREFIX = 1024
MOST = 3

F32 = jnp.float32
BF16 = jnp.bfloat16


def chip_swap(array, tensor_count):
    return lax.ppermute(array, "tensor", [(t, t ^ 1) for t in range(tensor_count)])


def shift(array, down, right, rows, columns):
    pairs = [
        (y * columns + x, (y + down) % rows * columns + (x + right) % columns)
        for y in range(rows)
        for x in range(columns)
    ]
    return lax.ppermute(array, "expert", pairs)


def ordered(pieces, index):
    count = len(pieces)
    return [lax.select_n((index - place) % count, *pieces) for place in range(count)]


def along_z(array, groups):
    return lax.all_to_all(
        array, "tensor", split_axis=0, concat_axis=0, tiled=True, axis_index_groups=groups
    )


def attend(queries, keys_values, prefix_len, kv_index):
    step_rows = queries.shape[0]
    per_device = queries.shape[1] // HD
    cached = lax.dynamic_index_in_dim(keys_values[0], kv_index, 0, keepdims=False)
    key_rows = cached[:, :HD]
    value_rows = cached[:, HD:]
    context = cached.shape[0]
    query_rows = queries.reshape(step_rows, per_device, HD)
    scores = jnp.einsum("nhd,cd->hnc", query_rows, key_rows, preferred_element_type=F32) / math.sqrt(HD)
    columns = jnp.arange(context, dtype=jnp.int32)[None, :]
    positions = jnp.arange(step_rows, dtype=jnp.int32)[:, None]
    visible = ((columns < prefix_len[0]) | (columns >= PREFIX) & (columns - PREFIX <= positions))[None]
    highest = jnp.max(jnp.where(visible, scores, -1e30), axis=-1, keepdims=True)
    weights = jnp.exp(jnp.where(visible, scores - highest, -1e30))
    summed = jnp.sum(weights, axis=-1)
    blended = jnp.einsum("hnc,cd->nhd", weights.astype(BF16), value_rows, preferred_element_type=F32)
    attended = (blended / jnp.transpose(summed)[:, :, None]).astype(BF16)
    return attended.reshape(step_rows, per_device * HD)


def shards(
    queries,
    keys_values,
    prefix_len,
    out_proj,
    residual,
    norm_gain,
    expert_ids,
    route_weights,
    w_gate,
    w_up,
    w_down,
):
    tensor_count = lax.axis_size("tensor")
    expert_count = lax.axis_size("expert")
    tensor_index = lax.axis_index("tensor")
    chips = tensor_count // 2
    core = tensor_index % 2
    same_core = [[2 * z + c for z in range(chips)] for c in range(2)]
    per_device = queries.shape[1] // HD
    width = residual.shape[1]
    half_rows = chips * TOK_DEV

    gate_other = chip_swap(w_gate[0], tensor_count)
    up_other = chip_swap(w_up[0], tensor_count)
    down_other = chip_swap(w_down[0], tensor_count)

    slot_index = tensor_index // HSPLIT
    slot_count = tensor_count // HSPLIT
    capacity = chips * MOST
    ids = expert_ids.reshape(chips, 2, TOK_DEV, TOPK)
    ids = lax.dynamic_index_in_dim(ids, core, 1, keepdims=False)
    gains = route_weights.reshape(chips, 2, TOK_DEV, TOPK)
    gains = lax.dynamic_index_in_dim(gains, core, 1, keepdims=False)
    wanted = jnp.arange(expert_count, dtype=jnp.int32) * slot_count + slot_index
    named = ids[:, :, :, None] == wanted
    hits = jnp.sum(named.astype(jnp.int32), axis=2)
    weight = jnp.sum(jnp.where(named, gains[:, :, :, None].astype(F32), 0.0), axis=2)
    earlier = (jnp.arange(TOK_DEV)[:, None] > jnp.arange(TOK_DEV)[None, :]).astype(BF16)
    rank = jnp.einsum("nm,zmj->znj", earlier, hits.astype(BF16), preferred_element_type=F32)
    position = jnp.arange(chips, dtype=jnp.int32)[:, None, None] * MOST + rank.astype(jnp.int32)
    position = jnp.where(hits > 0, position, -1).reshape(half_rows, expert_count)
    weight = weight.reshape(half_rows, expert_count)
    slots = jnp.arange(capacity, dtype=jnp.int32)
    pick = (position.T[:, None, :] == slots[None, :, None]).astype(BF16)
    pick = pick.reshape(expert_count * capacity, half_rows)
    combine = jnp.where(position[:, :, None] == slots[None, None, :], weight[:, :, None], 0.0)
    combine = combine.astype(BF16).reshape(half_rows, expert_count * capacity)

    side_y = side_x = math.isqrt(expert_count)
    expert_index = lax.axis_index("expert")
    place_y, place_x = expert_index // side_x, expert_index % side_x
    part_width = out_proj.shape[1]
    blocks = [out_proj] + [shift(out_proj, d, 0, side_y, side_x) for d in range(1, side_y)]
    projection = jnp.concatenate(ordered(blocks, place_y), axis=1)

    attended = attend(queries, keys_values, prefix_len, tensor_index * per_device // (HEADS // KVH))
    attended = attended.reshape(chips, 2, TOK_DEV, per_device * HD)
    attended = [lax.dynamic_index_in_dim(attended, c, 1, keepdims=False) for c in (1 - core, core)]
    attended = jnp.stack(attended).reshape(2, half_rows, per_device * HD)
    pieces = [attended] + [shift(attended, 0, d, side_y, side_x) for d in range(1, side_x)]
    rows_away = jnp.concatenate([piece[0] for piece in pieces], axis=0)
    rows_here = jnp.concatenate([piece[1] for piece in pieces], axis=0)
    part_away = jnp.dot(rows_away, projection, preferred_element_type=F32).astype(BF16)
    part_away = chip_swap(part_away, tensor_count)
    part_here = jnp.dot(rows_here, projection, preferred_element_type=F32).astype(BF16)
    chip_part = (part_here.astype(F32) + part_away.astype(F32)).astype(BF16)
    chip_part = chip_part.reshape(side_x, chips, TOK_DEV, side_y * part_width)
    chip_part = jnp.transpose(chip_part, (1, 0, 2, 3))
    chip_part, pick, combine, gate_other, up_other, down_other, residual, norm_gain = lax.optimization_barrier(
        (chip_part, pick, combine, gate_other, up_other, down_other, residual, norm_gain)
    )
    head_parts = along_z(chip_part, same_core)
    sums = jnp.sum(head_parts.astype(F32), axis=0).astype(BF16)
    sums = [sums[0]] + [shift(sums[d], 0, -d, side_y, side_x) for d in range(1, side_x)]
    sums = [one.reshape(TOK_DEV, side_y, part_width) for one in sums]
    sums = [sums[0]] + sums[:0:-1]
    head_sum = jnp.stack(ordered(sums, place_x), axis=2).reshape(TOK_DEV, width)
    hidden_state = (residual.astype(F32) + head_sum.astype(F32)).astype(BF16)

    values = hidden_state.astype(F32)
    factor = lax.rsqrt(jnp.mean(values * values, axis=-1, keepdims=True) + 1e-06)
    normed = (values * factor * norm_gain[None, :]).astype(BF16)
    normed_half = along_z(jnp.broadcast_to(normed[None], (chips,) + normed.shape), same_core)

    outgoing = jnp.dot(pick, normed_half.reshape(half_rows, width), preferred_element_type=F32).astype(BF16)
    arrived = lax.all_to_all(
        outgoing.reshape(expert_count, capacity, width), "expert", split_axis=0, concat_axis=0, tiled=True
    )
    rows = arrived.reshape(expert_count * capacity, width)

    def inner_of(gate, up):
        gate_val = jnp.dot(rows, gate, preferred_element_type=F32)
        up_val = jnp.dot(rows, up, preferred_element_type=F32)
        return (jax.nn.silu(gate_val) * up_val).astype(BF16)

    result = jnp.dot(inner_of(w_gate[0], w_up[0]), w_down[0], preferred_element_type=F32)
    result = result + jnp.dot(inner_of(gate_other, up_other), down_other, preferred_element_type=F32)
    result = result.astype(BF16).reshape(expert_count, capacity, width)
    returned = lax.all_to_all(result, "expert", split_axis=0, concat_axis=0, tiled=True)
    expert_part = jnp.dot(combine, returned.reshape(expert_count * capacity, width), preferred_element_type=F32)
    expert_parts = along_z(expert_part.astype(BF16).reshape(chips, TOK_DEV, width), same_core)
    expert_sum = jnp.sum(expert_parts.astype(F32), axis=0)
    return (hidden_state.astype(F32) + expert_sum).astype(BF16)


def solution(mesh):
    return jax.shard_map(
        shards,
        mesh=mesh,
        in_specs=(
            P("expert", "tensor"),
            P("expert", None, None, None),
            P("expert"),
            P("tensor", "expert"),
            P(("expert", "tensor"), None),
            P(),
            P("expert", None),
            P("expert", None),
            P(("expert", "tensor"), None, None),
            P(("expert", "tensor"), None, None),
            P(("expert", "tensor"), None, None),
        ),
        out_specs=P(("expert", "tensor"), None),
        check_vma=False,
    )
```

```python
import math

import jax
import jax.numpy as jnp
from jax import lax
from jax.experimental import pallas as pl
from jax.experimental.pallas import tpu as pltpu
from jax.sharding import PartitionSpec as P

HEADS = 64
KVH = 4
HD = 128
TOPK = 8
HSPLIT = 4
TOK_DEV = 16
PREFIX = 1024
MOST = 3

F32 = jnp.float32
BF16 = jnp.bfloat16


def chip_swap(array, tensor_count):
    return lax.ppermute(array, "tensor", [(t, t ^ 1) for t in range(tensor_count)])


def shift(array, down, right, rows, columns):
    pairs = [
        (y * columns + x, (y + down) % rows * columns + (x + right) % columns)
        for y in range(rows)
        for x in range(columns)
    ]
    return lax.ppermute(array, "expert", pairs)


def ordered(pieces, index):
    count = len(pieces)
    return [lax.select_n((index - place) % count, *pieces) for place in range(count)]


def along_z(array, groups):
    return lax.all_to_all(
        array, "tensor", split_axis=0, concat_axis=0, tiled=True, axis_index_groups=groups
    )


def experts_kernel(rows, gate_a, up_a, gate_b, up_b, down_a, down_b, out, wide, tall, total, inner, wide_sems, tall_sems):
    hidden = gate_a.shape[1]
    depth = rows.shape[1]
    steps = wide_sems.shape[0]
    chunk = depth // steps

    def wide_copy(step, place):
        span = pl.ds(pl.multiple_of(step * chunk, chunk), chunk)
        source = (gate_a, gate_b, up_a, up_b)[place]
        target = wide.at[span, pl.ds(place * hidden, hidden)]
        return pltpu.make_async_copy(source.at[span, :], target, wide_sems.at[step, place])

    def tall_copy(place):
        target = tall.at[pl.ds(place * hidden, hidden), :]
        return pltpu.make_async_copy((down_a, down_b)[place], target, tall_sems.at[place])

    for step in range(steps):
        for place in range(4):
            wide_copy(step, place).start()
    for place in range(2):
        tall_copy(place).start()
    total[...] = jnp.zeros_like(total)

    def multiply(step, carry):
        for place in range(4):
            wide_copy(step, place).wait()
        span = pl.ds(pl.multiple_of(step * chunk, chunk), chunk)
        total[...] += jnp.dot(rows[:, span], wide[span, :], preferred_element_type=F32)
        return carry

    lax.fori_loop(0, steps, multiply, 0)
    value = total[:, : 2 * hidden]
    inner[...] = (value / (1.0 + jnp.exp(-value)) * total[:, 2 * hidden :]).astype(BF16)
    for place in range(2):
        tall_copy(place).wait()

    def project(step, carry):
        span = pl.ds(pl.multiple_of(step * chunk, chunk), chunk)
        out[:, span] = jnp.dot(inner[...], tall[:, span], preferred_element_type=F32).astype(BF16)
        return carry

    lax.fori_loop(0, steps, project, 0)


def experts(rows, gate_a, up_a, down_a, gate_b, up_b, down_b):
    count, depth = rows.shape
    hidden = gate_a.shape[1]
    steps = 4
    whole = pl.BlockSpec(memory_space=pltpu.VMEM)
    return pl.pallas_call(
        experts_kernel,
        in_specs=[whole] + [pl.BlockSpec(memory_space=pl.ANY)] * 6,
        out_specs=whole,
        out_shape=jax.ShapeDtypeStruct((count, depth), BF16),
        scratch_shapes=[
            pltpu.VMEM((depth, 4 * hidden), BF16),
            pltpu.VMEM((2 * hidden, depth), BF16),
            pltpu.VMEM((count, 4 * hidden), F32),
            pltpu.VMEM((count, 2 * hidden), BF16),
            pltpu.SemaphoreType.DMA((steps, 4)),
            pltpu.SemaphoreType.DMA((2,)),
        ],
        compiler_params=pltpu.CompilerParams(vmem_limit_bytes=44 * 1024 * 1024),
        cost_estimate=pl.CostEstimate(
            flops=12 * count * depth * hidden,
            bytes_accessed=12 * hidden * depth + 4 * count * depth,
            transcendentals=2 * count * hidden,
        ),
    )(rows, gate_a, up_a, gate_b, up_b, down_a, down_b)


def attend(queries, keys_values, prefix_len, kv_index):
    step_rows = queries.shape[0]
    per_device = queries.shape[1] // HD
    cached = lax.dynamic_index_in_dim(keys_values[0], kv_index, 0, keepdims=False)
    key_rows = cached[:, :HD]
    value_rows = cached[:, HD:]
    context = cached.shape[0]
    query_rows = queries.reshape(step_rows, per_device, HD)
    scores = jnp.einsum("nhd,cd->hnc", query_rows, key_rows, preferred_element_type=F32) / math.sqrt(HD)
    columns = jnp.arange(context, dtype=jnp.int32)[None, :]
    positions = jnp.arange(step_rows, dtype=jnp.int32)[:, None]
    visible = ((columns < prefix_len[0]) | (columns >= PREFIX) & (columns - PREFIX <= positions))[None]
    highest = jnp.max(jnp.where(visible, scores, -1e30), axis=-1, keepdims=True)
    weights = jnp.exp(jnp.where(visible, scores - highest, -1e30))
    summed = jnp.sum(weights, axis=-1)
    blended = jnp.einsum("hnc,cd->nhd", weights.astype(BF16), value_rows, preferred_element_type=F32)
    attended = (blended / jnp.transpose(summed)[:, :, None]).astype(BF16)
    return attended.reshape(step_rows, per_device * HD)


def shards(
    queries,
    keys_values,
    prefix_len,
    out_proj,
    residual,
    norm_gain,
    expert_ids,
    route_weights,
    w_gate,
    w_up,
    w_down,
):
    tensor_count = lax.axis_size("tensor")
    expert_count = lax.axis_size("expert")
    tensor_index = lax.axis_index("tensor")
    chips = tensor_count // 2
    core = tensor_index % 2
    same_core = [[2 * z + c for z in range(chips)] for c in range(2)]
    per_device = queries.shape[1] // HD
    width = residual.shape[1]
    half_rows = chips * TOK_DEV

    gate_other = chip_swap(w_gate[0], tensor_count)
    up_other = chip_swap(w_up[0], tensor_count)
    down_other = chip_swap(w_down[0], tensor_count)

    slot_index = tensor_index // HSPLIT
    slot_count = tensor_count // HSPLIT
    capacity = chips * MOST
    ids = expert_ids.reshape(chips, 2, TOK_DEV, TOPK)
    ids = lax.dynamic_index_in_dim(ids, core, 1, keepdims=False)
    gains = route_weights.reshape(chips, 2, TOK_DEV, TOPK)
    gains = lax.dynamic_index_in_dim(gains, core, 1, keepdims=False)
    wanted = jnp.arange(expert_count, dtype=jnp.int32) * slot_count + slot_index
    named = ids[:, :, :, None] == wanted
    hits = jnp.sum(named.astype(jnp.int32), axis=2)
    weight = jnp.sum(jnp.where(named, gains[:, :, :, None].astype(F32), 0.0), axis=2)
    earlier = (jnp.arange(TOK_DEV)[:, None] > jnp.arange(TOK_DEV)[None, :]).astype(BF16)
    rank = jnp.einsum("nm,zmj->znj", earlier, hits.astype(BF16), preferred_element_type=F32)
    position = jnp.arange(chips, dtype=jnp.int32)[:, None, None] * MOST + rank.astype(jnp.int32)
    position = jnp.where(hits > 0, position, -1).reshape(half_rows, expert_count)
    weight = weight.reshape(half_rows, expert_count)
    slots = jnp.arange(capacity, dtype=jnp.int32)
    pick = (position.T[:, None, :] == slots[None, :, None]).astype(BF16)
    pick = pick.reshape(expert_count * capacity, half_rows)
    combine = jnp.where(position[:, :, None] == slots[None, None, :], weight[:, :, None], 0.0)
    combine = combine.astype(BF16).reshape(half_rows, expert_count * capacity)

    side_y = side_x = math.isqrt(expert_count)
    expert_index = lax.axis_index("expert")
    place_y, place_x = expert_index // side_x, expert_index % side_x
    part_width = out_proj.shape[1]
    blocks = [out_proj] + [shift(out_proj, d, 0, side_y, side_x) for d in range(1, side_y)]
    attended = attend(queries, keys_values, prefix_len, tensor_index * per_device // (HEADS // KVH))
    attended, blocks, gate_other, up_other, down_other = lax.optimization_barrier(
        (attended, blocks, gate_other, up_other, down_other)
    )
    projection = jnp.concatenate(ordered(blocks, place_y), axis=1)
    attended = attended.reshape(chips, 2, TOK_DEV, per_device * HD)
    attended = [lax.dynamic_index_in_dim(attended, c, 1, keepdims=False) for c in (1 - core, core)]
    attended = jnp.stack(attended).reshape(2, half_rows, per_device * HD)
    pieces = [attended] + [shift(attended, 0, d, side_y, side_x) for d in range(1, side_x)]
    rows_away = jnp.concatenate([piece[0] for piece in pieces], axis=0)
    rows_here = jnp.concatenate([piece[1] for piece in pieces], axis=0)
    part_away = jnp.dot(rows_away, projection, preferred_element_type=F32).astype(BF16)
    part_away = chip_swap(part_away, tensor_count)
    part_here = jnp.dot(rows_here, projection, preferred_element_type=F32).astype(BF16)
    chip_part = (part_here.astype(F32) + part_away.astype(F32)).astype(BF16)
    chip_part = chip_part.reshape(side_x, chips, TOK_DEV, side_y * part_width)
    chip_part = jnp.transpose(chip_part, (1, 0, 2, 3))
    chip_part, pick, combine, residual, norm_gain = lax.optimization_barrier(
        (chip_part, pick, combine, residual, norm_gain)
    )
    head_parts = along_z(chip_part, same_core)
    sums = jnp.sum(head_parts.astype(F32), axis=0).astype(BF16)
    sums = [sums[0]] + [shift(sums[d], 0, -d, side_y, side_x) for d in range(1, side_x)]
    sums = [one.reshape(TOK_DEV, side_y, part_width) for one in sums]
    sums = [sums[0]] + sums[:0:-1]
    head_sum = jnp.stack(ordered(sums, place_x), axis=2).reshape(TOK_DEV, width)
    hidden_state = (residual.astype(F32) + head_sum.astype(F32)).astype(BF16)

    values = hidden_state.astype(F32)
    factor = lax.rsqrt(jnp.mean(values * values, axis=-1, keepdims=True) + 1e-06)
    normed = (values * factor * norm_gain[None, :]).astype(BF16)
    normed_half = along_z(jnp.broadcast_to(normed[None], (chips,) + normed.shape), same_core)

    outgoing = jnp.dot(pick, normed_half.reshape(half_rows, width), preferred_element_type=F32).astype(BF16)
    arrived = lax.all_to_all(
        outgoing.reshape(expert_count, capacity, width), "expert", split_axis=0, concat_axis=0, tiled=True
    )
    rows = arrived.reshape(expert_count * capacity, width)

    result = experts(rows, w_gate[0], w_up[0], w_down[0], gate_other, up_other, down_other)
    result = result.reshape(expert_count, capacity, width)
    returned = lax.all_to_all(result, "expert", split_axis=0, concat_axis=0, tiled=True)
    expert_part = jnp.dot(combine, returned.reshape(expert_count * capacity, width), preferred_element_type=F32)
    expert_parts = along_z(expert_part.astype(BF16).reshape(chips, TOK_DEV, width), same_core)
    expert_sum = jnp.sum(expert_parts.astype(F32), axis=0)
    return (hidden_state.astype(F32) + expert_sum).astype(BF16)


def solution(mesh):
    return jax.shard_map(
        shards,
        mesh=mesh,
        in_specs=(
            P("expert", "tensor"),
            P("expert", None, None, None),
            P("expert"),
            P("tensor", "expert"),
            P(("expert", "tensor"), None),
            P(),
            P("expert", None),
            P("expert", None),
            P(("expert", "tensor"), None, None),
            P(("expert", "tensor"), None, None),
            P(("expert", "tensor"), None, None),
        ),
        out_specs=P(("expert", "tensor"), None),
        check_vma=False,
    )
```

```python
import math

import jax
import jax.numpy as jnp
from jax import lax
from jax.experimental import pallas as pl
from jax.experimental.pallas import tpu as pltpu
from jax.sharding import PartitionSpec as P

HEADS = 64
KVH = 4
HD = 128
TOPK = 8
HSPLIT = 4
TOK_DEV = 16
PREFIX = 1024
MOST = 3

F32 = jnp.float32
BF16 = jnp.bfloat16


def chip_swap(array, tensor_count):
    return lax.ppermute(array, "tensor", [(t, t ^ 1) for t in range(tensor_count)])


def shift(array, down, right, rows, columns):
    pairs = [
        (y * columns + x, (y + down) % rows * columns + (x + right) % columns)
        for y in range(rows)
        for x in range(columns)
    ]
    return lax.ppermute(array, "expert", pairs)


def ordered(pieces, index):
    count = len(pieces)
    return [lax.select_n((index - place) % count, *pieces) for place in range(count)]


def along_z(array, groups):
    return lax.all_to_all(
        array, "tensor", split_axis=0, concat_axis=0, tiled=True, axis_index_groups=groups
    )


def experts_kernel(rows, gate_a, up_a, gate_b, up_b, down_a, down_b, out, wide, tall, total, inner, wide_sems, tall_sems):
    hidden = gate_a.shape[1]
    depth = rows.shape[1]
    steps = wide_sems.shape[0]
    chunk = depth // steps

    def wide_copy(step, place):
        span = pl.ds(pl.multiple_of(step * chunk, chunk), chunk)
        source = (gate_a, gate_b, up_a, up_b)[place]
        target = wide.at[span, pl.ds(place * hidden, hidden)]
        return pltpu.make_async_copy(source.at[span, :], target, wide_sems.at[step, place])

    def tall_copy(place):
        target = tall.at[pl.ds(place * hidden, hidden), :]
        return pltpu.make_async_copy((down_a, down_b)[place], target, tall_sems.at[place])

    for step in range(steps):
        for place in range(4):
            wide_copy(step, place).start()
    for place in range(2):
        tall_copy(place).start()
    total[...] = jnp.zeros_like(total)

    def multiply(step, carry):
        for place in range(4):
            wide_copy(step, place).wait()
        span = pl.ds(pl.multiple_of(step * chunk, chunk), chunk)
        total[...] += jnp.dot(rows[:, span], wide[span, :], preferred_element_type=F32)
        return carry

    lax.fori_loop(0, steps, multiply, 0)
    value = total[:, : 2 * hidden]
    inner[...] = (value / (1.0 + jnp.exp(-value)) * total[:, 2 * hidden :]).astype(BF16)
    for place in range(2):
        tall_copy(place).wait()

    def project(step, carry):
        span = pl.ds(pl.multiple_of(step * chunk, chunk), chunk)
        out[:, span] = jnp.dot(inner[...], tall[:, span], preferred_element_type=F32).astype(BF16)
        return carry

    lax.fori_loop(0, steps, project, 0)


def experts(rows, gate_a, up_a, down_a, gate_b, up_b, down_b):
    count, depth = rows.shape
    hidden = gate_a.shape[1]
    steps = 4
    whole = pl.BlockSpec(memory_space=pltpu.VMEM)
    return pl.pallas_call(
        experts_kernel,
        in_specs=[whole] + [pl.BlockSpec(memory_space=pl.ANY)] * 6,
        out_specs=whole,
        out_shape=jax.ShapeDtypeStruct((count, depth), BF16),
        scratch_shapes=[
            pltpu.VMEM((depth, 4 * hidden), BF16),
            pltpu.VMEM((2 * hidden, depth), BF16),
            pltpu.VMEM((count, 4 * hidden), F32),
            pltpu.VMEM((count, 2 * hidden), BF16),
            pltpu.SemaphoreType.DMA((steps, 4)),
            pltpu.SemaphoreType.DMA((2,)),
        ],
        compiler_params=pltpu.CompilerParams(vmem_limit_bytes=44 * 1024 * 1024),
        cost_estimate=pl.CostEstimate(
            flops=12 * count * depth * hidden,
            bytes_accessed=12 * hidden * depth + 4 * count * depth,
            transcendentals=2 * count * hidden,
        ),
    )(rows, gate_a, up_a, gate_b, up_b, down_a, down_b)


def attend_kernel(scalars, queries, cached, out):
    rows = queries.shape[0]
    key, value = cached[0, 0, :, :HD], cached[0, 0, :, HD:]
    old_column = lax.broadcasted_iota(jnp.int32, (1, PREFIX), 1)
    live = old_column < scalars[1]
    step = (rows, key.shape[0] - PREFIX)
    causal = lax.broadcasted_iota(jnp.int32, step, 1) <= lax.broadcasted_iota(jnp.int32, step, 0)
    scale = 1.0 / (math.log(2.0) * math.sqrt(HD))
    contract = (((1,), (1,)), ((), ()))
    for head in range(queries.shape[1] // HD):
        span = slice(head * HD, (head + 1) * HD)
        query = queries[:, span]
        old = lax.dot_general(query, key[:PREFIX], contract, preferred_element_type=F32)
        new = lax.dot_general(query, key[PREFIX:], contract, preferred_element_type=F32)
        old = jnp.where(live, old, -1e30)
        new = jnp.where(causal, new, -1e30)
        highest = jnp.maximum(jnp.max(old, axis=-1, keepdims=True), jnp.max(new, axis=-1, keepdims=True))
        old = jnp.exp2((old - highest) * scale)
        new = jnp.exp2((new - highest) * scale)
        total = jnp.sum(old, axis=-1, keepdims=True) + jnp.sum(new, axis=-1, keepdims=True)
        blended = jnp.dot(old.astype(BF16), value[:PREFIX], preferred_element_type=F32)
        blended = blended + jnp.dot(new.astype(BF16), value[PREFIX:], preferred_element_type=F32)
        attended = (blended / total).reshape(rows // (2 * TOK_DEV), 2, TOK_DEV, HD)
        even, odd = attended[:, 0], attended[:, 1]
        first = scalars[2] == 0
        out[0, :, :, span] = jnp.where(first, odd, even).astype(BF16)
        out[1, :, :, span] = jnp.where(first, even, odd).astype(BF16)


def attend(scalars, queries, keys_values):
    rows, width = queries.shape
    context = keys_values.shape[2]
    shape = (2, rows // (2 * TOK_DEV), TOK_DEV, width)
    return pl.pallas_call(
        attend_kernel,
        grid_spec=pltpu.PrefetchScalarGridSpec(
            num_scalar_prefetch=1,
            grid=(1,),
            in_specs=[
                pl.BlockSpec((rows, width), lambda s, scalars: (0, 0)),
                pl.BlockSpec((1, 1, context, 2 * HD), lambda s, scalars: (0, scalars[0], 0, 0)),
            ],
            out_specs=pl.BlockSpec(shape, lambda s, scalars: (0, 0, 0, 0)),
        ),
        out_shape=jax.ShapeDtypeStruct(shape, BF16),
        compiler_params=pltpu.CompilerParams(vmem_limit_bytes=40 * 1024 * 1024),
        cost_estimate=pl.CostEstimate(
            flops=4 * rows * width * context,
            bytes_accessed=4 * rows * width + 4 * context * HD,
            transcendentals=rows * (width // HD) * context,
        ),
    )(scalars, queries, keys_values)


def shards(
    queries,
    keys_values,
    prefix_len,
    out_proj,
    residual,
    norm_gain,
    expert_ids,
    route_weights,
    w_gate,
    w_up,
    w_down,
):
    tensor_count = lax.axis_size("tensor")
    expert_count = lax.axis_size("expert")
    tensor_index = lax.axis_index("tensor")
    chips = tensor_count // 2
    core = tensor_index % 2
    same_core = [[2 * z + c for z in range(chips)] for c in range(2)]
    per_device = queries.shape[1] // HD
    width = residual.shape[1]
    half_rows = chips * TOK_DEV

    slot_index = tensor_index // HSPLIT
    slot_count = tensor_count // HSPLIT
    capacity = chips * MOST
    ids = expert_ids.reshape(chips, 2, TOK_DEV, TOPK)
    ids = lax.dynamic_index_in_dim(ids, core, 1, keepdims=False)
    gains = route_weights.reshape(chips, 2, TOK_DEV, TOPK)
    gains = lax.dynamic_index_in_dim(gains, core, 1, keepdims=False)
    wanted = jnp.arange(expert_count, dtype=jnp.int32) * slot_count + slot_index
    named = ids[:, :, :, None] == wanted
    hits = jnp.sum(named.astype(jnp.int32), axis=2)
    weight = jnp.sum(jnp.where(named, gains[:, :, :, None].astype(F32), 0.0), axis=2)
    earlier = (jnp.arange(TOK_DEV)[:, None] > jnp.arange(TOK_DEV)[None, :]).astype(BF16)
    rank = jnp.einsum("nm,zmj->znj", earlier, hits.astype(BF16), preferred_element_type=F32)
    position = jnp.arange(chips, dtype=jnp.int32)[:, None, None] * MOST + rank.astype(jnp.int32)
    position = jnp.where(hits > 0, position, -1).reshape(half_rows, expert_count)
    weight = weight.reshape(half_rows, expert_count)
    slots = jnp.arange(capacity, dtype=jnp.int32)
    pick = (position.T[:, None, :] == slots[None, :, None]).astype(BF16)
    pick = pick.reshape(expert_count * capacity, half_rows)
    combine = jnp.where(position[:, :, None] == slots[None, None, :], weight[:, :, None], 0.0)
    combine = combine.astype(BF16).reshape(half_rows, expert_count * capacity)

    side_y = side_x = math.isqrt(expert_count)
    expert_index = lax.axis_index("expert")
    place_y, place_x = expert_index // side_x, expert_index % side_x
    part_width = out_proj.shape[1]
    blocks = [out_proj] + [shift(out_proj, d, 0, side_y, side_x) for d in range(1, side_y)]
    kv_index = tensor_index * per_device // (HEADS // KVH)
    scalars = jnp.stack([kv_index, prefix_len[0], core]).astype(jnp.int32)
    scalars, gate_own, up_own, down_own = lax.optimization_barrier((scalars, w_gate[0], w_up[0], w_down[0]))
    gate_other = chip_swap(gate_own, tensor_count)
    up_other = chip_swap(up_own, tensor_count)
    attended = attend(scalars, queries, keys_values)
    attended, blocks, gate_other, up_other, down_own = lax.optimization_barrier(
        (attended, blocks, gate_other, up_other, down_own)
    )
    down_other = chip_swap(down_own, tensor_count)
    projection = jnp.concatenate(ordered(blocks, place_y), axis=1)
    pieces = [attended] + [shift(attended, 0, d, side_y, side_x) for d in range(1, side_x)]
    pieces, projection, pick, combine, down_other = lax.optimization_barrier(
        (pieces, projection, pick, combine, down_other)
    )
    rows_away = jnp.stack([piece[0] for piece in pieces], axis=1).reshape(-1, per_device * HD)
    rows_here = jnp.stack([piece[1] for piece in pieces], axis=1).reshape(-1, per_device * HD)
    part_away = jnp.dot(rows_away, projection, preferred_element_type=F32).astype(BF16)
    part_away = chip_swap(part_away, tensor_count)
    part_here = jnp.dot(rows_here, projection, preferred_element_type=F32).astype(BF16)
    chip_part = (part_here.astype(F32) + part_away.astype(F32)).astype(BF16)
    chip_part = chip_part.reshape(chips, side_x, TOK_DEV, -1)
    chip_part, residual, norm_gain = lax.optimization_barrier((chip_part, residual, norm_gain))
    head_parts = along_z(chip_part, same_core)
    sums = jnp.sum(head_parts.astype(F32), axis=0).astype(BF16)
    sums = [sums[0]] + [shift(sums[d], 0, -d, side_y, side_x) for d in range(1, side_x)]
    sums = [one.reshape(TOK_DEV, side_y, part_width) for one in sums]
    sums = [sums[0]] + sums[:0:-1]
    head_sum = jnp.stack(ordered(sums, place_x), axis=2).reshape(TOK_DEV, width)
    hidden_state = (residual.astype(F32) + head_sum.astype(F32)).astype(BF16)

    values = hidden_state.astype(F32)
    factor = lax.rsqrt(jnp.mean(values * values, axis=-1, keepdims=True) + 1e-06)
    normed = (values * factor * norm_gain[None, :]).astype(BF16)
    normed_half = along_z(jnp.broadcast_to(normed[None], (chips,) + normed.shape), same_core)

    outgoing = jnp.dot(pick, normed_half.reshape(half_rows, width), preferred_element_type=F32).astype(BF16)
    arrived = lax.all_to_all(
        outgoing.reshape(expert_count, capacity, width), "expert", split_axis=0, concat_axis=0, tiled=True
    )
    rows = arrived.reshape(expert_count * capacity, width)

    result = experts(rows, gate_own, up_own, down_own, gate_other, up_other, down_other)
    result = result.reshape(expert_count, capacity, width)
    returned = lax.all_to_all(result, "expert", split_axis=0, concat_axis=0, tiled=True)
    expert_part = jnp.dot(combine, returned.reshape(expert_count * capacity, width), preferred_element_type=F32)
    expert_parts = along_z(expert_part.astype(BF16).reshape(chips, TOK_DEV, width), same_core)
    expert_sum = jnp.sum(expert_parts.astype(F32), axis=0)
    return (hidden_state.astype(F32) + expert_sum).astype(BF16)


def solution(mesh):
    return jax.shard_map(
        shards,
        mesh=mesh,
        in_specs=(
            P("expert", "tensor"),
            P("expert", None, None, None),
            P("expert"),
            P("tensor", "expert"),
            P(("expert", "tensor"), None),
            P(),
            P("expert", None),
            P("expert", None),
            P(("expert", "tensor"), None, None),
            P(("expert", "tensor"), None, None),
            P(("expert", "tensor"), None, None),
        ),
        out_specs=P(("expert", "tensor"), None),
        check_vma=False,
    )
```

```python
import math

import jax
import jax.numpy as jnp
from jax import lax
from jax.experimental import pallas as pl
from jax.experimental.pallas import tpu as pltpu
from jax.sharding import PartitionSpec as P

HEADS = 64
KVH = 4
HD = 128
TOPK = 8
HSPLIT = 4
TOK_DEV = 16
PREFIX = 1024
MOST = 3

F32 = jnp.float32
BF16 = jnp.bfloat16


def chip_swap(array, tensor_count):
    return lax.ppermute(array, "tensor", [(t, t ^ 1) for t in range(tensor_count)])


def shift(array, down, right, rows, columns):
    pairs = [
        (y * columns + x, (y + down) % rows * columns + (x + right) % columns)
        for y in range(rows)
        for x in range(columns)
    ]
    return lax.ppermute(array, "expert", pairs)


def ordered(pieces, index):
    count = len(pieces)
    return [lax.select_n((index - place) % count, *pieces) for place in range(count)]


def along_z(array, groups):
    return lax.all_to_all(
        array, "tensor", split_axis=0, concat_axis=0, tiled=True, axis_index_groups=groups
    )


def experts_kernel(rows, gate_a, up_a, gate_b, up_b, down_a, down_b, out, wide, tall, total, inner, wide_sems, tall_sems):
    hidden = gate_a.shape[1]
    depth = rows.shape[1]
    steps = wide_sems.shape[0]
    chunk = depth // steps

    def wide_copy(step, place):
        span = pl.ds(pl.multiple_of(step * chunk, chunk), chunk)
        source = (gate_a, gate_b, up_a, up_b)[place]
        target = wide.at[span, pl.ds(place * hidden, hidden)]
        return pltpu.make_async_copy(source.at[span, :], target, wide_sems.at[step, place])

    def tall_copy(place):
        target = tall.at[pl.ds(place * hidden, hidden), :]
        return pltpu.make_async_copy((down_a, down_b)[place], target, tall_sems.at[place])

    for step in range(steps):
        for place in range(4):
            wide_copy(step, place).start()
    for place in range(2):
        tall_copy(place).start()
    total[...] = jnp.zeros_like(total)

    def multiply(step, carry):
        for place in range(4):
            wide_copy(step, place).wait()
        span = pl.ds(pl.multiple_of(step * chunk, chunk), chunk)
        total[...] += jnp.dot(rows[:, span], wide[span, :], preferred_element_type=F32)
        return carry

    lax.fori_loop(0, steps, multiply, 0)
    value = total[:, : 2 * hidden]
    inner[...] = (value / (1.0 + jnp.exp(-value)) * total[:, 2 * hidden :]).astype(BF16)
    for place in range(2):
        tall_copy(place).wait()

    def project(step, carry):
        span = pl.ds(pl.multiple_of(step * chunk, chunk), chunk)
        out[:, span] = jnp.dot(inner[...], tall[:, span], preferred_element_type=F32).astype(BF16)
        return carry

    lax.fori_loop(0, steps, project, 0)


def experts(rows, gate_a, up_a, down_a, gate_b, up_b, down_b):
    count, depth = rows.shape
    hidden = gate_a.shape[1]
    steps = 4
    whole = pl.BlockSpec(memory_space=pltpu.VMEM)
    return pl.pallas_call(
        experts_kernel,
        in_specs=[whole] + [pl.BlockSpec(memory_space=pl.ANY)] * 6,
        out_specs=whole,
        out_shape=jax.ShapeDtypeStruct((count, depth), BF16),
        scratch_shapes=[
            pltpu.VMEM((depth, 4 * hidden), BF16),
            pltpu.VMEM((2 * hidden, depth), BF16),
            pltpu.VMEM((count, 4 * hidden), F32),
            pltpu.VMEM((count, 2 * hidden), BF16),
            pltpu.SemaphoreType.DMA((steps, 4)),
            pltpu.SemaphoreType.DMA((2,)),
        ],
        compiler_params=pltpu.CompilerParams(vmem_limit_bytes=44 * 1024 * 1024),
        cost_estimate=pl.CostEstimate(
            flops=12 * count * depth * hidden,
            bytes_accessed=12 * hidden * depth + 4 * count * depth,
            transcendentals=2 * count * hidden,
        ),
    )(rows, gate_a, up_a, gate_b, up_b, down_a, down_b)


def attend_kernel(scalars, queries, cached, out):
    rows = queries.shape[0]
    key, value = cached[0, 0, :, :HD], cached[0, 0, :, HD:]
    old_column = lax.broadcasted_iota(jnp.int32, (1, PREFIX), 1)
    live = old_column < scalars[1]
    step = (rows, key.shape[0] - PREFIX)
    causal = lax.broadcasted_iota(jnp.int32, step, 1) <= lax.broadcasted_iota(jnp.int32, step, 0)
    scale = 1.0 / (math.log(2.0) * math.sqrt(HD))
    contract = (((1,), (1,)), ((), ()))
    for head in range(queries.shape[1] // HD):
        span = slice(head * HD, (head + 1) * HD)
        query = queries[:, span]
        old = lax.dot_general(query, key[:PREFIX], contract, preferred_element_type=F32)
        new = lax.dot_general(query, key[PREFIX:], contract, preferred_element_type=F32)
        old = jnp.where(live, old, -1e30)
        new = jnp.where(causal, new, -1e30)
        highest = jnp.maximum(jnp.max(old, axis=-1, keepdims=True), jnp.max(new, axis=-1, keepdims=True))
        old = jnp.exp2((old - highest) * scale)
        new = jnp.exp2((new - highest) * scale)
        total = jnp.sum(old, axis=-1, keepdims=True) + jnp.sum(new, axis=-1, keepdims=True)
        blended = jnp.dot(old.astype(BF16), value[:PREFIX], preferred_element_type=F32)
        blended = blended + jnp.dot(new.astype(BF16), value[PREFIX:], preferred_element_type=F32)
        attended = (blended / total).reshape(rows // (2 * TOK_DEV), 2, TOK_DEV, HD)
        even, odd = attended[:, 0], attended[:, 1]
        first = scalars[2] == 0
        out[0, :, :, span] = jnp.where(first, odd, even).astype(BF16)
        out[1, :, :, span] = jnp.where(first, even, odd).astype(BF16)


def attend(scalars, queries, keys_values):
    rows, width = queries.shape
    context = keys_values.shape[2]
    shape = (2, rows // (2 * TOK_DEV), TOK_DEV, width)
    return pl.pallas_call(
        attend_kernel,
        grid_spec=pltpu.PrefetchScalarGridSpec(
            num_scalar_prefetch=1,
            grid=(1,),
            in_specs=[
                pl.BlockSpec((rows, width), lambda s, scalars: (0, 0)),
                pl.BlockSpec((1, 1, context, 2 * HD), lambda s, scalars: (0, scalars[0], 0, 0)),
            ],
            out_specs=pl.BlockSpec(shape, lambda s, scalars: (0, 0, 0, 0)),
        ),
        out_shape=jax.ShapeDtypeStruct(shape, BF16),
        compiler_params=pltpu.CompilerParams(vmem_limit_bytes=40 * 1024 * 1024),
        cost_estimate=pl.CostEstimate(
            flops=4 * rows * width * context,
            bytes_accessed=4 * rows * width + 4 * context * HD,
            transcendentals=rows * (width // HD) * context,
        ),
    )(scalars, queries, keys_values)


def shards(
    queries,
    keys_values,
    prefix_len,
    out_proj,
    residual,
    norm_gain,
    expert_ids,
    route_weights,
    w_gate,
    w_up,
    w_down,
):
    tensor_count = lax.axis_size("tensor")
    expert_count = lax.axis_size("expert")
    tensor_index = lax.axis_index("tensor")
    chips = tensor_count // 2
    core = tensor_index % 2
    same_core = [[2 * z + c for z in range(chips)] for c in range(2)]
    per_device = queries.shape[1] // HD
    width = residual.shape[1]
    half_rows = chips * TOK_DEV

    slot_index = tensor_index // HSPLIT
    slot_count = tensor_count // HSPLIT
    capacity = chips * MOST
    ids = expert_ids.reshape(chips, 2, TOK_DEV, TOPK)
    ids = lax.dynamic_index_in_dim(ids, core, 1, keepdims=False)
    gains = route_weights.reshape(chips, 2, TOK_DEV, TOPK)
    gains = lax.dynamic_index_in_dim(gains, core, 1, keepdims=False)
    wanted = jnp.arange(expert_count, dtype=jnp.int32) * slot_count + slot_index
    named = ids[:, :, :, None] == wanted
    hits = jnp.sum(named.astype(jnp.int32), axis=2)
    weight = jnp.sum(jnp.where(named, gains[:, :, :, None].astype(F32), 0.0), axis=2)
    earlier = (jnp.arange(TOK_DEV)[:, None] > jnp.arange(TOK_DEV)[None, :]).astype(BF16)
    rank = jnp.einsum("nm,zmj->znj", earlier, hits.astype(BF16), preferred_element_type=F32)
    position = jnp.arange(chips, dtype=jnp.int32)[:, None, None] * MOST + rank.astype(jnp.int32)
    position = jnp.where(hits > 0, position, -1).reshape(half_rows, expert_count)
    weight = weight.reshape(half_rows, expert_count)
    slots = jnp.arange(capacity, dtype=jnp.int32)
    pick = (position.T[:, None, :] == slots[None, :, None]).astype(BF16)
    pick = pick.reshape(expert_count * capacity, half_rows)
    combine = jnp.where(position[:, :, None] == slots[None, None, :], weight[:, :, None], 0.0)
    combine = combine.astype(BF16).reshape(half_rows, expert_count * capacity)

    side_y = side_x = math.isqrt(expert_count)
    expert_index = lax.axis_index("expert")
    place_y, place_x = expert_index // side_x, expert_index % side_x
    part_width = out_proj.shape[1]
    blocks = [out_proj] + [shift(out_proj, d, 0, side_y, side_x) for d in range(1, side_y)]
    kv_index = tensor_index * per_device // (HEADS // KVH)
    scalars = jnp.stack([kv_index, prefix_len[0], core]).astype(jnp.int32)
    scalars, gate_own, up_own, down_own = lax.optimization_barrier((scalars, w_gate[0], w_up[0], w_down[0]))
    gate_other = chip_swap(gate_own, tensor_count)
    attended = attend(scalars, queries, keys_values)
    attended, blocks, gate_other, up_own, down_own, pick = lax.optimization_barrier(
        (attended, blocks, gate_other, up_own, down_own, pick)
    )
    up_other = chip_swap(up_own, tensor_count)
    down_other = chip_swap(down_own, tensor_count)
    projection = jnp.concatenate(ordered(blocks, place_y), axis=1)
    pieces = [attended] + [shift(attended, 0, d, side_y, side_x) for d in range(1, side_x)]
    pieces, projection, combine, up_other, down_other = lax.optimization_barrier(
        (pieces, projection, combine, up_other, down_other)
    )
    rows_away = jnp.stack([piece[0] for piece in pieces], axis=1).reshape(-1, per_device * HD)
    rows_here = jnp.stack([piece[1] for piece in pieces], axis=1).reshape(-1, per_device * HD)
    part_away = jnp.dot(rows_away, projection, preferred_element_type=F32).astype(BF16)
    part_away = chip_swap(part_away, tensor_count)
    part_here = jnp.dot(rows_here, projection, preferred_element_type=F32).astype(BF16)
    chip_part = (part_here.astype(F32) + part_away.astype(F32)).astype(BF16)
    chip_part = chip_part.reshape(chips, side_x, TOK_DEV, -1)
    chip_part, residual, norm_gain = lax.optimization_barrier((chip_part, residual, norm_gain))
    head_parts = along_z(chip_part, same_core)
    sums = jnp.sum(head_parts.astype(F32), axis=0).astype(BF16)
    sums = [sums[0]] + [shift(sums[d], 0, -d, side_y, side_x) for d in range(1, side_x)]
    sums = [one.reshape(TOK_DEV, side_y, part_width) for one in sums]
    sums = [sums[0]] + sums[:0:-1]
    head_sum = jnp.stack(ordered(sums, place_x), axis=2).reshape(TOK_DEV, width)
    hidden_state = (residual.astype(F32) + head_sum.astype(F32)).astype(BF16)

    values = hidden_state.astype(F32)
    factor = lax.rsqrt(jnp.mean(values * values, axis=-1, keepdims=True) + 1e-06)
    normed = (values * factor * norm_gain[None, :]).astype(BF16)
    normed_half = along_z(jnp.broadcast_to(normed[None], (chips,) + normed.shape), same_core)

    outgoing = jnp.dot(pick, normed_half.reshape(half_rows, width), preferred_element_type=F32).astype(BF16)
    arrived = lax.all_to_all(
        outgoing.reshape(expert_count, capacity, width), "expert", split_axis=0, concat_axis=0, tiled=True
    )
    rows = arrived.reshape(expert_count * capacity, width)

    result = experts(rows, gate_own, up_own, down_own, gate_other, up_other, down_other)
    result = result.reshape(expert_count, capacity, width)
    returned = lax.all_to_all(result, "expert", split_axis=0, concat_axis=0, tiled=True)
    expert_part = jnp.dot(combine, returned.reshape(expert_count * capacity, width), preferred_element_type=F32)
    expert_parts = along_z(expert_part.astype(BF16).reshape(chips, TOK_DEV, width), same_core)
    expert_sum = jnp.sum(expert_parts.astype(F32), axis=0)
    return (hidden_state.astype(F32) + expert_sum).astype(BF16)


def solution(mesh):
    return jax.shard_map(
        shards,
        mesh=mesh,
        in_specs=(
            P("expert", "tensor"),
            P("expert", None, None, None),
            P("expert"),
            P("tensor", "expert"),
            P(("expert", "tensor"), None),
            P(),
            P("expert", None),
            P("expert", None),
            P(("expert", "tensor"), None, None),
            P(("expert", "tensor"), None, None),
            P(("expert", "tensor"), None, None),
        ),
        out_specs=P(("expert", "tensor"), None),
        check_vma=False,
    )
```

```python
import math

import jax
import jax.numpy as jnp
from jax import lax
from jax.experimental import pallas as pl
from jax.experimental.pallas import tpu as pltpu
from jax.sharding import PartitionSpec as P

HEADS = 64
KVH = 4
HD = 128
TOPK = 8
HSPLIT = 4
TOK_DEV = 16
PREFIX = 1024
MOST = 3

F32 = jnp.float32
BF16 = jnp.bfloat16


def chip_swap(array, tensor_count):
    return lax.ppermute(array, "tensor", [(t, t ^ 1) for t in range(tensor_count)])


def shift(array, down, right, rows, columns):
    pairs = [
        (y * columns + x, (y + down) % rows * columns + (x + right) % columns)
        for y in range(rows)
        for x in range(columns)
    ]
    return lax.ppermute(array, "expert", pairs)


def ordered(pieces, index):
    count = len(pieces)
    return [lax.select_n((index - place) % count, *pieces) for place in range(count)]


def along_z(array, groups):
    return lax.all_to_all(
        array, "tensor", split_axis=0, concat_axis=0, tiled=True, axis_index_groups=groups
    )


def experts_kernel(rows, gate_a, up_a, gate_b, up_b, down_a, down_b, out, wide, tall, total, inner, wide_sems, tall_sems):
    hidden = gate_a.shape[1]
    depth = rows.shape[1]
    steps = wide_sems.shape[0]
    chunk = depth // steps

    def wide_copy(step, place):
        span = pl.ds(step * chunk, chunk)
        source = (gate_a, gate_b, up_a, up_b)[place]
        target = wide.at[span, pl.ds(place * hidden, hidden)]
        return pltpu.make_async_copy(source.at[span, :], target, wide_sems.at[step, place])

    def tall_copy(place):
        target = tall.at[pl.ds(place * hidden, hidden), :]
        return pltpu.make_async_copy((down_a, down_b)[place], target, tall_sems.at[place])

    for step in range(steps):
        for place in range(4):
            wide_copy(step, place).start()
    for place in range(2):
        tall_copy(place).start()

    def multiply(step, first):
        for place in range(4):
            wide_copy(step, place).wait()
        span = pl.ds(step * chunk, chunk)
        term = jnp.dot(rows[:, span], wide[span, :], preferred_element_type=F32)
        total[...] = term if first else total[...] + term

    for step in range(steps):
        multiply(step, step == 0)
    value = total[:, : 2 * hidden]
    inner[...] = (value / (1.0 + jnp.exp(-value)) * total[:, 2 * hidden :]).astype(BF16)
    for place in range(2):
        tall_copy(place).wait()

    def project(step, carry):
        span = pl.ds(pl.multiple_of(step * chunk, chunk), chunk)
        out[:, span] = jnp.dot(inner[...], tall[:, span], preferred_element_type=F32).astype(BF16)
        return carry

    lax.fori_loop(0, steps, project, 0)


def experts(rows, gate_a, up_a, down_a, gate_b, up_b, down_b):
    count, depth = rows.shape
    hidden = gate_a.shape[1]
    steps = 2
    whole = pl.BlockSpec(memory_space=pltpu.VMEM)
    return pl.pallas_call(
        experts_kernel,
        in_specs=[whole] + [pl.BlockSpec(memory_space=pl.ANY)] * 6,
        out_specs=whole,
        out_shape=jax.ShapeDtypeStruct((count, depth), BF16),
        scratch_shapes=[
            pltpu.VMEM((depth, 4 * hidden), BF16),
            pltpu.VMEM((2 * hidden, depth), BF16),
            pltpu.VMEM((count, 4 * hidden), F32),
            pltpu.VMEM((count, 2 * hidden), BF16),
            pltpu.SemaphoreType.DMA((steps, 4)),
            pltpu.SemaphoreType.DMA((2,)),
        ],
        compiler_params=pltpu.CompilerParams(vmem_limit_bytes=44 * 1024 * 1024),
        cost_estimate=pl.CostEstimate(
            flops=12 * count * depth * hidden,
            bytes_accessed=12 * hidden * depth + 4 * count * depth,
            transcendentals=2 * count * hidden,
        ),
    )(rows, gate_a, up_a, gate_b, up_b, down_a, down_b)


def attend_kernel(scalars, queries, cached, out):
    rows = queries.shape[0]
    key, value = cached[0, 0, :, :HD], cached[0, 0, :, HD:]
    old_column = lax.broadcasted_iota(jnp.int32, (1, PREFIX), 1)
    live = old_column < scalars[1]
    step = (rows, key.shape[0] - PREFIX)
    causal = lax.broadcasted_iota(jnp.int32, step, 1) <= lax.broadcasted_iota(jnp.int32, step, 0)
    scale = 1.0 / (math.log(2.0) * math.sqrt(HD))
    contract = (((1,), (1,)), ((), ()))
    for head in range(queries.shape[1] // HD):
        span = slice(head * HD, (head + 1) * HD)
        query = queries[:, span]
        old = lax.dot_general(query, key[:PREFIX], contract, preferred_element_type=F32)
        new = lax.dot_general(query, key[PREFIX:], contract, preferred_element_type=F32)
        old = jnp.where(live, old, -1e30)
        new = jnp.where(causal, new, -1e30)
        highest = jnp.maximum(jnp.max(old, axis=-1, keepdims=True), jnp.max(new, axis=-1, keepdims=True))
        old = jnp.exp2((old - highest) * scale)
        new = jnp.exp2((new - highest) * scale)
        total = jnp.sum(old, axis=-1, keepdims=True) + jnp.sum(new, axis=-1, keepdims=True)
        blended = jnp.dot(old.astype(BF16), value[:PREFIX], preferred_element_type=F32)
        blended = blended + jnp.dot(new.astype(BF16), value[PREFIX:], preferred_element_type=F32)
        attended = (blended / total).reshape(rows // (2 * TOK_DEV), 2, TOK_DEV, HD)
        even, odd = attended[:, 0], attended[:, 1]
        first = scalars[2] == 0
        out[0, :, :, span] = jnp.where(first, odd, even).astype(BF16)
        out[1, :, :, span] = jnp.where(first, even, odd).astype(BF16)


def attend(scalars, queries, keys_values):
    rows, width = queries.shape
    context = keys_values.shape[2]
    shape = (2, rows // (2 * TOK_DEV), TOK_DEV, width)
    return pl.pallas_call(
        attend_kernel,
        grid_spec=pltpu.PrefetchScalarGridSpec(
            num_scalar_prefetch=1,
            grid=(1,),
            in_specs=[
                pl.BlockSpec((rows, width), lambda s, scalars: (0, 0)),
                pl.BlockSpec((1, 1, context, 2 * HD), lambda s, scalars: (0, scalars[0], 0, 0)),
            ],
            out_specs=pl.BlockSpec(shape, lambda s, scalars: (0, 0, 0, 0)),
        ),
        out_shape=jax.ShapeDtypeStruct(shape, BF16),
        compiler_params=pltpu.CompilerParams(vmem_limit_bytes=40 * 1024 * 1024),
        cost_estimate=pl.CostEstimate(
            flops=4 * rows * width * context,
            bytes_accessed=4 * rows * width + 4 * context * HD,
            transcendentals=rows * (width // HD) * context,
        ),
    )(scalars, queries, keys_values)


def shards(
    queries,
    keys_values,
    prefix_len,
    out_proj,
    residual,
    norm_gain,
    expert_ids,
    route_weights,
    w_gate,
    w_up,
    w_down,
):
    tensor_count = lax.axis_size("tensor")
    expert_count = lax.axis_size("expert")
    tensor_index = lax.axis_index("tensor")
    chips = tensor_count // 2
    core = tensor_index % 2
    same_core = [[2 * z + c for z in range(chips)] for c in range(2)]
    per_device = queries.shape[1] // HD
    width = residual.shape[1]
    half_rows = chips * TOK_DEV

    slot_index = tensor_index // HSPLIT
    slot_count = tensor_count // HSPLIT
    capacity = chips * MOST
    ids = expert_ids.reshape(chips, 2, TOK_DEV, TOPK)
    ids = lax.dynamic_index_in_dim(ids, core, 1, keepdims=False)
    gains = route_weights.reshape(chips, 2, TOK_DEV, TOPK)
    gains = lax.dynamic_index_in_dim(gains, core, 1, keepdims=False)
    wanted = jnp.arange(expert_count, dtype=jnp.int32) * slot_count + slot_index
    named = ids[:, :, :, None] == wanted
    hits = jnp.sum(named.astype(jnp.int32), axis=2)
    weight = jnp.sum(jnp.where(named, gains[:, :, :, None].astype(F32), 0.0), axis=2)
    earlier = (jnp.arange(TOK_DEV)[:, None] > jnp.arange(TOK_DEV)[None, :]).astype(BF16)
    rank = jnp.einsum("nm,zmj->znj", earlier, hits.astype(BF16), preferred_element_type=F32)
    position = jnp.arange(chips, dtype=jnp.int32)[:, None, None] * MOST + rank.astype(jnp.int32)
    position = jnp.where(hits > 0, position, -1).reshape(half_rows, expert_count)
    weight = weight.reshape(half_rows, expert_count)
    slots = jnp.arange(capacity, dtype=jnp.int32)
    pick = (position.T[:, None, :] == slots[None, :, None]).astype(BF16)
    pick = pick.reshape(expert_count * capacity, half_rows)
    combine = jnp.where(position[:, :, None] == slots[None, None, :], weight[:, :, None], 0.0)
    combine = combine.astype(BF16).reshape(half_rows, expert_count * capacity)

    side_y = side_x = math.isqrt(expert_count)
    expert_index = lax.axis_index("expert")
    place_y, place_x = expert_index // side_x, expert_index % side_x
    part_width = out_proj.shape[1]
    blocks = [out_proj] + [shift(out_proj, d, 0, side_y, side_x) for d in range(1, side_y)]
    kv_index = tensor_index * per_device // (HEADS // KVH)
    scalars = jnp.stack([kv_index, prefix_len[0], core]).astype(jnp.int32)
    scalars, gate_own, up_own, down_own = lax.optimization_barrier((scalars, w_gate[0], w_up[0], w_down[0]))
    gate_other = chip_swap(gate_own, tensor_count)
    attended = attend(scalars, queries, keys_values)
    attended, blocks, gate_other, up_own, down_own, pick = lax.optimization_barrier(
        (attended, blocks, gate_other, up_own, down_own, pick)
    )
    up_other = chip_swap(up_own, tensor_count)
    down_other = chip_swap(down_own, tensor_count)
    projection = jnp.concatenate(ordered(blocks, place_y), axis=1)
    pieces = [attended] + [shift(attended, 0, d, side_y, side_x) for d in range(1, side_x)]
    pieces, projection, combine, up_other, down_other = lax.optimization_barrier(
        (pieces, projection, combine, up_other, down_other)
    )
    rows_away = jnp.stack([piece[0] for piece in pieces], axis=1).reshape(-1, per_device * HD)
    rows_here = jnp.stack([piece[1] for piece in pieces], axis=1).reshape(-1, per_device * HD)
    part_away = jnp.dot(rows_away, projection, preferred_element_type=F32).astype(BF16)
    part_away = chip_swap(part_away, tensor_count)
    part_here = jnp.dot(rows_here, projection, preferred_element_type=F32).astype(BF16)
    chip_part = (part_here.astype(F32) + part_away.astype(F32)).astype(BF16)
    chip_part = chip_part.reshape(chips, side_x, TOK_DEV, -1)
    chip_part, residual, norm_gain = lax.optimization_barrier((chip_part, residual, norm_gain))
    head_parts = along_z(chip_part, same_core)
    sums = jnp.sum(head_parts.astype(F32), axis=0).astype(BF16)
    sums = [sums[0]] + [shift(sums[d], 0, -d, side_y, side_x) for d in range(1, side_x)]
    sums = [one.reshape(TOK_DEV, side_y, part_width) for one in sums]
    sums = [sums[0]] + sums[:0:-1]
    head_sum = jnp.stack(ordered(sums, place_x), axis=2).reshape(TOK_DEV, width)
    hidden_state = (residual.astype(F32) + head_sum.astype(F32)).astype(BF16)

    values = hidden_state.astype(F32)
    factor = lax.rsqrt(jnp.mean(values * values, axis=-1, keepdims=True) + 1e-06)
    normed = (values * factor * norm_gain[None, :]).astype(BF16)
    normed_half = along_z(jnp.broadcast_to(normed[None], (chips,) + normed.shape), same_core)

    outgoing = jnp.dot(pick, normed_half.reshape(half_rows, width), preferred_element_type=F32).astype(BF16)
    arrived = lax.all_to_all(
        outgoing.reshape(expert_count, capacity, width), "expert", split_axis=0, concat_axis=0, tiled=True
    )
    rows = arrived.reshape(expert_count * capacity, width)

    result = experts(rows, gate_own, up_own, down_own, gate_other, up_other, down_other)
    result = result.reshape(expert_count, capacity, width)
    returned = lax.all_to_all(result, "expert", split_axis=0, concat_axis=0, tiled=True)
    expert_part = jnp.dot(combine, returned.reshape(expert_count * capacity, width), preferred_element_type=F32)
    expert_parts = along_z(expert_part.astype(BF16).reshape(chips, TOK_DEV, width), same_core)
    expert_sum = jnp.sum(expert_parts.astype(F32), axis=0)
    return (hidden_state.astype(F32) + expert_sum).astype(BF16)


def solution(mesh):
    return jax.shard_map(
        shards,
        mesh=mesh,
        in_specs=(
            P("expert", "tensor"),
            P("expert", None, None, None),
            P("expert"),
            P("tensor", "expert"),
            P(("expert", "tensor"), None),
            P(),
            P("expert", None),
            P("expert", None),
            P(("expert", "tensor"), None, None),
            P(("expert", "tensor"), None, None),
            P(("expert", "tensor"), None, None),
        ),
        out_specs=P(("expert", "tensor"), None),
        check_vma=False,
    )
```
